32 devices in a mesh: groups: 2 (over x), ctx: 16 (over z, y, core).
Axes of the slice: x: 2, y: 2, z: 4, core: 2. Of those that a mesh axis runs over, the one named last changes fastest.
Arguments:
- query: bfloat16 [4096, 1536], P(('groups', 'ctx')), parts along dimension 0, may hold values from -5 to 5
- key_rows: bfloat16 [4096, 1536], P(('groups', 'ctx')), parts along dimension 0, may hold values from -5 to 5
- value: bfloat16 [4096, 1536], P(('groups', 'ctx')), parts along dimension 0, may hold values from -6 to 6
- grad_out: bfloat16 [4096, 1536], P(('groups', 'ctx')), parts along dimension 0, may hold values from -6 to 6
- kv_slots: int32 [16, 18], replicated, may hold values from -1 to 15, as said below
Outputs:
- out: bfloat16 [4096, 1536], P(('groups', 'ctx')), parts along dimension 0
- grad_query: bfloat16 [4096, 1536], P(('groups', 'ctx')), parts along dimension 0
- grad_key: bfloat16 [4096, 1536], P(('groups', 'ctx')), parts along dimension 0
- grad_value: bfloat16 [4096, 1536], P(('groups', 'ctx')), parts along dimension 0
The draws below stay inside these ranges and needn't reach their ends.
There are 2 independent parts, one for each index of `groups`. The reference program is written for one: setup_inputs(seed, part) draws one part's arguments, and reference() takes and returns one part's arrays. A program takes and returns all parts, laid end to end along the dimension named above; an argument that names none is the same for every part. Nothing has to cross between parts.
Inputs may be any that keep to these rules, and one draw needn't show every extreme that they name: `kv_slots`: blocks are the tiles of two time planes of 4 x 2 tiles in raster order (plane, row, column). The row of block b lists, in a drawn order, b itself and a drawn subset of the blocks whose tile lies in either plane within one row and one column of b's tile; -1 fills the other entries. No block is listed twice in a row.
All inputs are finite; a program needn't handle non-finite values.
Results may differ from the reference program's by a relative error of at most 0.0065.
The reference program's roundings to bfloat16 on the way (of `weights` and `grad_scores`) count: a program that leaves them out, or rounds other values in their place, can miss the bound.
Values may be sent and summed in bfloat16 or wider, within the bound.
No kernel may reach another device: no remote copies, remote signals or barrier semaphores. Data moves between devices by JAX's collectives and lax.ppermute only.
A program may use at most 128 MiB of HBM per device.

```python
import jax
import jax.numpy as jnp
from jax import lax

HEADS = 12
HEAD = 128
BLOCK = 128
TILE_H = 4
KSLOT = 18
NBLK = 16
TOKENS = 2048
FEAT = 1536


def paired_fields(key):
    seeded = jax.random.fold_in(key, 11)
    first_key, second_key = jax.random.split(seeded, 2)
    features = HEADS * HEAD
    query_field = jnp.clip(jax.random.normal(first_key, (TOKENS, features), jnp.float32), -5.0, 5.0)
    key_field = jnp.clip(jax.random.normal(second_key, (TOKENS, features), jnp.float32), -5.0, 5.0)
    return (query_field, key_field)


def draw_query(key, part):
    return paired_fields(key)[0].astype(jnp.bfloat16)


def draw_key_rows(key, part):
    return paired_fields(key)[1].astype(jnp.bfloat16)


def draw_kv_slots(key, part):
    slot_ids = jnp.arange(NBLK, dtype=jnp.int32)
    tile_width = NBLK // (2 * TILE_H)
    plane_size = TILE_H * tile_width
    plane_of = slot_ids // plane_size
    row_of = slot_ids // tile_width % TILE_H
    column_of = slot_ids % tile_width
    columns_list = []
    for plane_step in (0, 1):
        for row_step in (-1, 0, 1):
            for col_step in (-1, 0, 1):
                other_plane = jnp.abs(plane_of - plane_step)
                row_new = row_of + row_step
                column_new = column_of + col_step
                inside = (row_new >= 0) & (row_new < TILE_H) & (column_new >= 0) & (column_new < tile_width)
                columns_list.append(jnp.where(inside, other_plane * plane_size + row_new * tile_width + column_new, -1))
    slot_table = jnp.stack(columns_list, axis=1).astype(jnp.int32)
    keep_draw = jax.random.randint(jax.random.fold_in(key, 5), (NBLK, KSLOT), 0, 4).astype(jnp.int32)
    is_self = (jnp.arange(KSLOT, dtype=jnp.int32) == 4)[None, :]
    keep = (keep_draw > 0) | is_self
    slot_table = jnp.where(keep, slot_table, -1).astype(jnp.int32)
    orders = jax.vmap(lambda row_key: jax.random.permutation(row_key, KSLOT))(jax.random.split(key, NBLK))
    return jnp.take_along_axis(slot_table, orders.astype(jnp.int32), axis=1).astype(jnp.int32)


def block_levels(own_key, extent, cuts, low, largest):
    def one(dim, parts):
        steps = jax.random.uniform(jax.random.fold_in(jax.random.fold_in(own_key, 6), dim), (parts,), jnp.float32, low / len(cuts), largest / len(cuts))
        return jnp.repeat(jnp.exp(steps), extent[dim] // parts).reshape((-1,) + (1,) * (len(extent) - dim - 1))

    factor_of = one(*cuts[0])
    for cut in cuts[1:]:
        factor_of = factor_of * one(*cut)
    return factor_of


def centred(own_key, dims, deviation, bound, pieces=(), held_as=jnp.bfloat16):
    array = deviation * jax.random.normal(own_key, dims, jnp.float32)
    if pieces:
        array = array * block_levels(own_key, dims, pieces, -0.22, 0.18)
    return jnp.clip(array, -bound, bound).astype(held_as)


def setup_inputs(seed: int = 0, part: int = 0) -> dict:
    seeds = jax.random.split(jax.random.key(seed), 6)
    part_splits = jax.random.split(jax.random.fold_in(seeds[5], part), 6)
    return {
        "query": draw_query(jax.random.fold_in(jax.random.fold_in(seeds[5], part), 71), part),
        "key_rows": draw_key_rows(jax.random.fold_in(jax.random.fold_in(seeds[5], part), 71), part),
        "value": centred(part_splits[2], (TOKENS, FEAT), 1.0, 6.0, ((0, 16),)),
        "grad_out": centred(part_splits[3], (TOKENS, FEAT), 1.0, 6.0, ((0, 16),)),
        "kv_slots": draw_kv_slots(jax.random.fold_in(seeds[5], 71), part),
    }


def block_scores(query_block, key_blocks, is_valid, scaling):
    scores = jnp.einsum("qhd,jkhd->hqjk", query_block.astype(jnp.float32), key_blocks.astype(jnp.float32)) * scaling
    return jnp.where(is_valid[None, None, :, None], scores, -1e30)


def reference(query, key_rows, value, grad_out, kv_slots):
    block_count = TOKENS // BLOCK
    query_blocks = query.reshape(block_count, BLOCK, HEADS, HEAD)
    key_blocks = key_rows.reshape(block_count, BLOCK, HEADS, HEAD)
    value_blocks = value.reshape(block_count, BLOCK, HEADS, HEAD)
    grad_blocks = grad_out.reshape(block_count, BLOCK, HEADS, HEAD)
    is_valid = kv_slots >= 0
    safe_slot = jnp.where(is_valid, kv_slots, 0).astype(jnp.int32)
    scaling = HEAD ** -0.5

    def forward(block_index):
        keys_here = key_blocks[safe_slot[block_index]]
        values_here = value_blocks[safe_slot[block_index]]
        scores = block_scores(query_blocks[block_index], keys_here, is_valid[block_index], scaling)
        peak_score = jnp.max(scores, axis=(2, 3), keepdims=True)
        log_norm = peak_score + jnp.log(jnp.sum(jnp.exp(scores - peak_score), axis=(2, 3), keepdims=True))
        weights = lax.optimization_barrier(jnp.exp(scores - log_norm).astype(jnp.bfloat16))
        mixed_rows = jnp.einsum("hqjk,jkhd->qhd", weights.astype(jnp.float32), values_here.astype(jnp.float32))
        return mixed_rows.astype(jnp.bfloat16), log_norm[:, :, 0, 0]

    out_blocks, log_norms = lax.map(forward, jnp.arange(block_count))
    delta_rows = jnp.sum(grad_blocks.astype(jnp.float32) * out_blocks.astype(jnp.float32), axis=3)

    def backward(carry, block_index):
        key_total, value_total = carry
        keys_here = key_blocks[safe_slot[block_index]]
        values_here = value_blocks[safe_slot[block_index]]
        scores = block_scores(query_blocks[block_index], keys_here, is_valid[block_index], scaling)
        weights = jnp.exp(scores - log_norms[block_index][:, :, None, None])
        weights_low = lax.optimization_barrier(weights.astype(jnp.bfloat16))
        grad_here = grad_blocks[block_index].astype(jnp.float32)
        grad_probs = jnp.einsum("qhd,jkhd->hqjk", grad_here, values_here.astype(jnp.float32))
        grad_scores = weights * (grad_probs - jnp.transpose(delta_rows[block_index])[:, :, None, None])
        grad_scores = lax.optimization_barrier(grad_scores.astype(jnp.bfloat16)).astype(jnp.float32)
        grad_query_block = (jnp.einsum("hqjk,jkhd->qhd", grad_scores, keys_here.astype(jnp.float32)) * scaling).astype(jnp.bfloat16)
        value_part = jnp.einsum("hqjk,qhd->jkhd", weights_low.astype(jnp.float32), grad_here)
        key_part = jnp.einsum("hqjk,qhd->jkhd", grad_scores, query_blocks[block_index].astype(jnp.float32)) * scaling
        keep = is_valid[block_index][:, None, None, None]
        key_total = key_total.at[safe_slot[block_index]].add(jnp.where(keep, key_part, 0.0))
        value_total = value_total.at[safe_slot[block_index]].add(jnp.where(keep, value_part, 0.0))
        return (key_total, value_total), grad_query_block

    zero_blocks = jnp.zeros((block_count, BLOCK, HEADS, HEAD), jnp.float32)
    (key_total, value_total), grad_query_blocks = lax.scan(backward, (zero_blocks, zero_blocks), jnp.arange(block_count))
    features = HEADS * HEAD
    return (out_blocks.reshape(TOKENS, features),
            grad_query_blocks.reshape(TOKENS, features),
            key_total.astype(jnp.bfloat16).reshape(TOKENS, features),
            value_total.astype(jnp.bfloat16).reshape(TOKENS, features))
```

```python
import functools

import jax
import jax.numpy as jnp
from jax import lax
from jax.experimental import pallas as pl
from jax.experimental.pallas import tpu as pltpu
from jax.sharding import PartitionSpec as P

HEADS = 12
HEAD = 128
BLOCK = 128
TILE_H = 4
PLANES = 2

head_batch = 4
masked_score = -1e30
log2_e = 1.4426950408889634


def nt_dot(left, right):
    return lax.dot_general(
        left, right, (((1,), (1,)), ((), ())), preferred_element_type=jnp.float32
    )


def nn_dot(left, right):
    return lax.dot_general(
        left, right, (((1,), (0,)), ((), ())), preferred_element_type=jnp.float32
    )


def key_rows_of(row):
    return jnp.maximum(row - 1, 0), jnp.minimum(row + 2, TILE_H)


def row_blocks(width, row):
    return [plane * TILE_H * width + row * width + col for plane in range(PLANES) for col in range(width)]


def query_places(width):
    return PLANES * TILE_H, width * BLOCK


def forward_kernel(width, kvq_ref, bias_ref, out_ref, log_ref, score_ref, vt_ref):
    blocks = PLANES * TILE_H * width
    steps, lanes = query_places(width)
    scale = HEAD ** (-0.5) * log2_e
    for block in range(blocks):
        vt_ref[block] = jnp.transpose(kvq_ref[block, 1])

    def step(place, _):
        row = place % TILE_H
        first = place * width
        queries = kvq_ref[pl.ds(first, width), 2].reshape(lanes, HEAD)
        low, high = key_rows_of(row)

        def scores_of(key_row, peak):
            for block in row_blocks(width, key_row):
                scores = nt_dot(kvq_ref[block, 0], queries) * scale
                scores = scores + bias_ref[block, place]
                score_ref[block] = scores
                peak = jnp.maximum(peak, jnp.max(scores.reshape(-1, 8, lanes), axis=0))
            return peak

        peak = lax.fori_loop(low, high, scores_of, jnp.full((8, lanes), masked_score, jnp.float32))
        peak = jnp.max(peak, axis=0, keepdims=True)

        def total_of(key_row, total):
            for block in row_blocks(width, key_row):
                power = jnp.exp2(score_ref[block] - peak)
                score_ref[block] = power
                total = total + jnp.sum(power.reshape(-1, 8, lanes), axis=0)
            return total

        total = lax.fori_loop(low, high, total_of, jnp.zeros((8, lanes), jnp.float32))
        total = jnp.sum(total, axis=0, keepdims=True)
        inverse = 1.0 / total
        log_ref[place] = jnp.broadcast_to(peak + jnp.log2(total), (8, lanes))

        def mixed_of(key_row, mixed):
            for block in row_blocks(width, key_row):
                weights = (score_ref[block] * inverse).astype(jnp.bfloat16)
                mixed = mixed + nn_dot(vt_ref[block], weights)
            return mixed

        mixed = lax.fori_loop(low, high, mixed_of, jnp.zeros((HEAD, lanes), jnp.float32))
        out_ref[pl.ds(first, width)] = (
            jnp.transpose(mixed).astype(jnp.bfloat16).reshape(width, BLOCK, HEAD)
        )
        return 0

    lax.fori_loop(0, steps, step, 0)


def backward_kernel(
    width, kvq_ref, grad_ref, out_ref, log_ref, bias_ref, terms_ref, kt_ref, key_acc, value_acc
):
    blocks = PLANES * TILE_H * width
    steps, lanes = query_places(width)
    factor = HEAD ** (-0.5)
    scale = factor * log2_e
    for block in range(blocks):
        kt_ref[block] = jnp.transpose(kvq_ref[block, 0])
    key_acc[...] = jnp.zeros_like(key_acc)
    value_acc[...] = jnp.zeros_like(value_acc)

    def step(place, _):
        row = place % TILE_H
        first = place * width
        queries = kvq_ref[pl.ds(first, width), 2].reshape(lanes, HEAD)
        grads = grad_ref[pl.ds(first, width)].reshape(lanes, HEAD)
        outs = out_ref[pl.ds(first, width)].reshape(lanes, HEAD)
        products = grads.astype(jnp.float32) * outs.astype(jnp.float32)
        delta = jnp.sum(jnp.transpose(products), axis=0, keepdims=True)
        log_row = log_ref[place][:1]
        low, high = key_rows_of(row)

        def one_row(key_row, total):
            for block in row_blocks(width, key_row):
                scores = nt_dot(kvq_ref[block, 0], queries) * scale
                scores = scores + bias_ref[block, place]
                weights = jnp.exp2(scores - log_row)
                grad_probs = nt_dot(kvq_ref[block, 1], grads)
                grad_scores = (weights * (grad_probs - delta)).astype(jnp.bfloat16)
                value_acc[block] += nn_dot(weights.astype(jnp.bfloat16), grads)
                key_acc[block] += nn_dot(grad_scores, queries)
                total = total + nn_dot(kt_ref[block], grad_scores)
            return total

        total = lax.fori_loop(low, high, one_row, jnp.zeros((HEAD, lanes), jnp.float32))
        terms_ref[pl.ds(first, width), 0] = (
            (jnp.transpose(total) * factor).astype(jnp.bfloat16).reshape(width, BLOCK, HEAD)
        )
        return 0

    lax.fori_loop(0, steps, step, 0)
    for block in range(blocks):
        terms_ref[block, 1] = (key_acc[block] * factor).astype(jnp.bfloat16)
        terms_ref[block, 2] = value_acc[block].astype(jnp.bfloat16)


def in_vmem(count):
    return [pl.BlockSpec(memory_space=pltpu.VMEM)] * count


def forward_head(width, kvq, bias):
    blocks = kvq.shape[0]
    steps, lanes = query_places(width)
    pairs = blocks * blocks * BLOCK * BLOCK
    return pl.pallas_call(
        functools.partial(forward_kernel, width),
        out_shape=(
            jax.ShapeDtypeStruct((blocks, BLOCK, HEAD), jnp.bfloat16),
            jax.ShapeDtypeStruct((steps, 8, lanes), jnp.float32),
        ),
        in_specs=in_vmem(2),
        out_specs=tuple(in_vmem(2)),
        scratch_shapes=[
            pltpu.VMEM((blocks, BLOCK, lanes), jnp.float32),
            pltpu.VMEM((blocks, HEAD, BLOCK), jnp.bfloat16),
        ],
        cost_estimate=pl.CostEstimate(
            flops=4 * pairs * HEAD, bytes_accessed=4 * kvq.size, transcendentals=pairs
        ),
        name="forward_head",
    )(kvq, bias)


def backward_head(width, kvq, grads, outs, logs, bias):
    blocks = kvq.shape[0]
    pairs = blocks * blocks * BLOCK * BLOCK
    return pl.pallas_call(
        functools.partial(backward_kernel, width),
        out_shape=jax.ShapeDtypeStruct((blocks, 3, BLOCK, HEAD), jnp.bfloat16),
        in_specs=in_vmem(5),
        out_specs=pl.BlockSpec(memory_space=pltpu.VMEM),
        scratch_shapes=[
            pltpu.VMEM((blocks, HEAD, BLOCK), jnp.bfloat16),
            pltpu.VMEM((blocks, BLOCK, HEAD), jnp.float32),
            pltpu.VMEM((blocks, BLOCK, HEAD), jnp.float32),
        ],
        cost_estimate=pl.CostEstimate(
            flops=10 * pairs * HEAD, bytes_accessed=8 * kvq.size, transcendentals=pairs
        ),
        name="backward_head",
    )(kvq, grads, outs, logs, bias)


def mask_bias(kv_slots, blocks, width):
    listed = jnp.any(
        kv_slots[:, :, None] == jnp.arange(blocks, dtype=jnp.int32)[None, None, :], axis=1
    )
    bias = jnp.where(jnp.transpose(listed), 0.0, masked_score).astype(jnp.float32)
    steps, lanes = query_places(width)
    bias = jnp.broadcast_to(bias[:, :, None], (blocks, blocks, BLOCK))
    return bias.reshape(blocks, steps, 1, lanes)


def by_head(tensors, devices):
    stacked = jnp.stack([tensor.reshape(BLOCK, HEADS, HEAD) for tensor in tensors])
    stacked = jnp.transpose(stacked, (2, 0, 1, 3))
    return jnp.pad(stacked, ((0, devices - HEADS), (0, 0), (0, 0), (0, 0)))


def to_tokens(received):
    return jnp.transpose(received[:HEADS], (1, 0, 2)).reshape(BLOCK, HEADS * HEAD)


def swap(value):
    return lax.all_to_all(value, "ctx", 0, 0, tiled=True)


def heads_body(query, key_rows, value, grad_out, kv_slots):
    devices = lax.axis_size("ctx")
    width = devices // (PLANES * TILE_H)
    bias = mask_bias(kv_slots, devices, width)
    kvq = swap(by_head((key_rows, value, query), devices))
    grads = swap(by_head((grad_out,), devices))[:, 0]
    outs, logs = forward_head(width, kvq, bias)
    out = to_tokens(swap(outs))
    terms = swap(backward_head(width, kvq, grads, outs, logs, bias))
    return (out, to_tokens(terms[:, 0]), to_tokens(terms[:, 1]), to_tokens(terms[:, 2]))


def from_behind(value, axis, by):
    count = lax.axis_size(axis)
    return lax.ppermute(value, axis, [(i, (i + by) % count) for i in range(count)])


def neighbour_offsets(devices, blocks, tile_width):
    plane_size = TILE_H * tile_width
    total_slots = devices * blocks
    offset_set = set()
    for plane_step in (0, 1):
        for row_step in (-1, 0, 1):
            for col_step in (-1, 0, 1):
                offset = (plane_step * plane_size + row_step * tile_width + col_step) % total_slots
                target = offset % total_slots // blocks
                if target > devices // 2:
                    target = target - devices
                if target != 0:
                    offset_set.add(target)
    return offset_set


def split_heads(tensor):
    return tensor.reshape(
        tensor.shape[0], HEADS // head_batch, head_batch, tensor.shape[1] // HEADS
    )


def pick_group(tensor, group_index):
    return lax.dynamic_index_in_dim(tensor, group_index, 1, keepdims=False)


def join_heads(stacked):
    return jnp.moveaxis(stacked, 0, 1).reshape(stacked.shape[1], -1)


def apply_mask(scores, block_mask):
    heads_here, row_total, col_total = scores.shape
    row_blocks, col_blocks = block_mask.shape
    shaped = scores.reshape(
        heads_here, row_blocks, row_total // row_blocks, col_blocks, col_total // col_blocks
    )
    shaped = jnp.where(block_mask[None, :, None, :, None], shaped, masked_score)
    return shaped.reshape(heads_here, row_total, col_total)


def forward_group(group_index, queries, keys, values, allowed, scaling):
    query_part = pick_group(queries, group_index)
    key_part = pick_group(keys, group_index)
    value_part = pick_group(values, group_index)
    scores = (
        jnp.einsum("qhd,khd->hqk", query_part, key_part, preferred_element_type=jnp.float32)
        * scaling
    )
    scores = apply_mask(scores, allowed)
    peak_score = jnp.max(scores, axis=2, keepdims=True)
    denominator = jnp.sum(jnp.exp(scores - peak_score), axis=2, keepdims=True)
    log_norm = peak_score + jnp.log(denominator)
    weights = jnp.exp(scores - log_norm).astype(jnp.bfloat16)
    mixed_rows = jnp.einsum("hqk,khd->qhd", weights, value_part, preferred_element_type=jnp.float32)
    return (mixed_rows, log_norm[:, :, 0])


def query_group(
    group_index, queries, keys, values, gradients, log_split, delta_split, allowed, scaling
):
    query_part = pick_group(queries, group_index)
    key_part = pick_group(keys, group_index)
    value_part = pick_group(values, group_index)
    grad_part = pick_group(gradients, group_index)
    log_part = jnp.transpose(pick_group(log_split, group_index))
    delta_part = jnp.transpose(pick_group(delta_split, group_index))
    scores = (
        jnp.einsum("qhd,khd->hqk", query_part, key_part, preferred_element_type=jnp.float32)
        * scaling
    )
    scores = apply_mask(scores, allowed)
    weights = jnp.exp(scores - log_part[:, :, None])
    grad_probs = jnp.einsum(
        "qhd,khd->hqk", grad_part, value_part, preferred_element_type=jnp.float32
    )
    grad_scores = (weights * (grad_probs - delta_part[:, :, None])).astype(jnp.bfloat16)
    return (
        jnp.einsum("hqk,khd->qhd", grad_scores, key_part, preferred_element_type=jnp.float32)
        * scaling
    )


def key_group(
    group_index, keys, values, queries, gradients, log_split, delta_split, back_mask, scaling
):
    key_part = pick_group(keys, group_index)
    value_part = pick_group(values, group_index)
    query_part = pick_group(queries, group_index)
    grad_part = pick_group(gradients, group_index)
    log_part = jnp.transpose(pick_group(log_split, group_index))
    delta_part = jnp.transpose(pick_group(delta_split, group_index))
    scores = (
        jnp.einsum("khd,chd->hkc", key_part, query_part, preferred_element_type=jnp.float32)
        * scaling
    )
    scores = apply_mask(scores, back_mask)
    weights = jnp.exp(scores - log_part[:, None, :])
    grad_probs = jnp.einsum(
        "khd,chd->hkc", value_part, grad_part, preferred_element_type=jnp.float32
    )
    grad_scores = (weights * (grad_probs - delta_part[:, None, :])).astype(jnp.bfloat16)
    grad_values = jnp.einsum(
        "hkc,chd->khd", weights.astype(jnp.bfloat16), grad_part, preferred_element_type=jnp.float32
    )
    grad_keys = (
        jnp.einsum("hkc,chd->khd", grad_scores, query_part, preferred_element_type=jnp.float32)
        * scaling
    )
    return (grad_keys, grad_values)


def neighbour_body(query, key_rows, value, grad_out, kv_slots):
    devices = lax.axis_size("ctx")
    device_index = lax.axis_index("ctx")
    row_count = query.shape[0]
    blocks = row_count // BLOCK
    tile_width = devices * blocks // (2 * TILE_H)
    offset_set = neighbour_offsets(devices, blocks, tile_width)
    visit_order = sorted(offset_set)
    distances = [0] + visit_order
    local_slots = jnp.arange(blocks, dtype=jnp.int32)
    cand_slots = jnp.concatenate(
        [(device_index + distance) % devices * blocks + local_slots for distance in distances]
    ).astype(jnp.int32)
    own_blocks = device_index * blocks + local_slots
    own_lists = lax.dynamic_slice_in_dim(kv_slots, device_index * blocks, blocks, 0)
    allowed = jnp.any(own_lists[:, :, None] == cand_slots[None, None, :], axis=1)
    cand_lists = jnp.take(kv_slots, cand_slots, axis=0)
    back_mask = jnp.any(cand_lists[None, :, :] == own_blocks[:, None, None], axis=2)
    scaling = HEAD ** (-0.5)
    groups = HEADS // head_batch
    group_ids = jnp.arange(groups)
    arrived = [from_behind((key_rows, value), "ctx", -distance) for distance in visit_order]
    cand_keys = split_heads(jnp.concatenate([key_rows] + [item[0] for item in arrived], axis=0))
    cand_values = split_heads(jnp.concatenate([value] + [item[1] for item in arrived], axis=0))
    queries = split_heads(query)
    mixed_all, norm_all = lax.map(
        lambda group_index: forward_group(
            group_index, queries, cand_keys, cand_values, allowed, scaling
        ),
        group_ids,
    )
    out = join_heads(mixed_all).astype(jnp.bfloat16)
    log_rows = jnp.transpose(norm_all.reshape(HEADS, row_count))
    delta_rows = jnp.sum(
        (grad_out.astype(jnp.float32) * out.astype(jnp.float32)).reshape(row_count, HEADS, -1),
        axis=2,
    )
    gradients = split_heads(grad_out)
    log_split = log_rows.reshape(row_count, groups, head_batch)
    delta_split = delta_rows.reshape(row_count, groups, head_batch)
    query_terms = lax.map(
        lambda group_index: query_group(
            group_index,
            queries,
            cand_keys,
            cand_values,
            gradients,
            log_split,
            delta_split,
            allowed,
            scaling,
        ),
        group_ids,
    )
    grad_query = join_heads(query_terms).astype(jnp.bfloat16)
    returned = [from_behind((query, grad_out), "ctx", -distance) for distance in visit_order]
    cand_queries = jnp.concatenate([query] + [item[0] for item in returned], axis=0)
    cand_grads = jnp.concatenate([grad_out] + [item[1] for item in returned], axis=0)
    row_terms = [from_behind((log_rows, delta_rows), "ctx", -distance) for distance in visit_order]
    cand_log = jnp.concatenate([log_rows] + [item[0] for item in row_terms], axis=0).reshape(
        -1, groups, head_batch
    )
    cand_delta = jnp.concatenate([delta_rows] + [item[1] for item in row_terms], axis=0).reshape(
        -1, groups, head_batch
    )
    own_keys = split_heads(key_rows)
    own_values = split_heads(value)
    split_queries = split_heads(cand_queries)
    split_grads = split_heads(cand_grads)
    key_terms, value_terms = lax.map(
        lambda group_index: key_group(
            group_index,
            own_keys,
            own_values,
            split_queries,
            split_grads,
            cand_log,
            cand_delta,
            back_mask,
            scaling,
        ),
        group_ids,
    )
    grad_key = join_heads(key_terms).astype(jnp.bfloat16)
    grad_value = join_heads(value_terms).astype(jnp.bfloat16)
    return (out, grad_query, grad_key, grad_value)


def solution(mesh):
    rows = P(("groups", "ctx"), None)
    devices = mesh.shape["ctx"]

    def body(query, *others):
        one_block = query.shape[0] == BLOCK and devices % (PLANES * TILE_H) == 0
        if one_block and HEADS <= devices <= 2 * HEADS:
            return heads_body(query, *others)
        return neighbour_body(query, *others)

    return jax.shard_map(
        body,
        mesh=mesh,
        in_specs=(rows, rows, rows, rows, P()),
        out_specs=(rows, rows, rows, rows),
        check_vma=False,
    )
```
